32 devices in a mesh: dp: 16 (over z, y, core), seq: 2 (over x).
Axes of the slice: x: 2, y: 2, z: 4, core: 2. Of those that a mesh axis runs over, the one named last changes fastest.
Arguments:
- inputs: bfloat16 [2, 16, 768, 256], P(None, 'dp', 'seq'), may hold values from -6 to 6
- lengths: int32 [2, 16], P(None, 'dp'), may hold values from 1 to 768, 9216 in all within a row
- cotangent: bfloat16 [2, 16, 768, 256], P(None, 'dp', 'seq'), may hold values from -6 to 6
- feed_in: bfloat16 [2, 256, 1024], P(None, None, ('dp', 'seq')), may hold values from -0.375 to 0.375
- feed_in_bias: bfloat16 [2, 1024], P(None, ('dp', 'seq')), may hold values from -3 to 3
- feed_out: bfloat16 [2, 1024, 256], P(None, ('dp', 'seq')), may hold values from -0.375 to 0.375
- attend_in: bfloat16 [4, 256, 256], P(None, None, ('dp', 'seq')), may hold values from -0.375 to 0.375
- attend_out: bfloat16 [256, 256], P(None, ('dp', 'seq')), may hold values from -1.5 to 1.5
- point_in: bfloat16 [256, 512], P(None, ('dp', 'seq')), may hold values from -0.375 to 0.375
- point_in_bias: bfloat16 [512], P(('dp', 'seq')), may hold values from -3 to 3
- depth_kernel: bfloat16 [31, 256], P(None, ('dp', 'seq')), may hold values from -1 to 1
- point_out: bfloat16 [256, 256], P(None, ('dp', 'seq')), may hold values from -0.5 to 0.5
- gains: bfloat16 [6, 256], P(None, ('dp', 'seq')), may hold values from 0.25 to 1.75
- biases: bfloat16 [14, 256], P(None, ('dp', 'seq')), may hold values from -3 to 3
Outputs:
- layer_out: bfloat16 [2, 16, 768, 256], P(None, 'dp', 'seq')
- input_grad: float32 [2, 16, 768, 256], P(None, 'dp', 'seq')
- feed_in_grad: float32 [2, 256, 1024], P(None, None, ('dp', 'seq'))
- feed_in_bias_grad: float32 [2, 1024], P(None, ('dp', 'seq'))
- feed_out_grad: float32 [2, 1024, 256], P(None, ('dp', 'seq'))
- attend_in_grad: float32 [4, 256, 256], P(None, None, ('dp', 'seq'))
- attend_out_grad: float32 [256, 256], P(None, ('dp', 'seq'))
- point_in_grad: float32 [256, 512], P(None, ('dp', 'seq'))
- point_in_bias_grad: float32 [512], P(('dp', 'seq'))
- depth_kernel_grad: float32 [31, 256], P(None, ('dp', 'seq'))
- point_out_grad: float32 [256, 256], P(None, ('dp', 'seq'))
- gains_grad: float32 [6, 256], P(None, ('dp', 'seq'))
- biases_grad: float32 [14, 256], P(None, ('dp', 'seq'))
The draws below stay inside these ranges and needn't reach their ends.
Inputs may be any that keep to these rules, and one draw needn't show every extreme that they name: Within each micro-batch the longest sequence has 768 tokens and the lengths sum to 9216.
All inputs are finite; a program needn't handle non-finite values. No bound on the sum of `lengths` on one device may be relied on, other than what follows from the above.
Results may differ from the reference program's by a relative error of at most 0.025.
Values may be sent and summed in bfloat16 or wider, within the bound.
No kernel may reach another device: no remote copies, remote signals or barrier semaphores. Data moves between devices by JAX's collectives and lax.ppermute only.
A program may use at most 192 MiB of HBM per device.

```python
import math
from functools import partial
import jax
import jax.numpy as jnp
import numpy as np
from jax import lax

D = 256
HEAD = 64
FF = 1024
KERNEL = 31
MICRO = 2
SEQ_LEN = 768
SEQUENCES = 16
VALID = 9216


def levels(own_key, shape, cuts, least, top_value):
    def one(axis_at, blocks):
        heights = jax.random.uniform(jax.random.fold_in(jax.random.fold_in(own_key, 6), axis_at), (blocks,), jnp.float32, least / len(cuts), top_value / len(cuts))
        return jnp.repeat(jnp.exp(heights), shape[axis_at] // blocks).reshape((-1,) + (1,) * (len(shape) - axis_at - 1))

    loudness = one(*cuts[0])
    for cut in cuts[1:]:
        loudness = loudness * one(*cut)
    return loudness


def profile(amount, total, most, slope):
    portions = [(1 << 20) // math.isqrt(rank ** slope) + 1 for rank in range(2, amount + 1)]
    rest, holding = total - most - (amount - 1), [1] * (amount - 1)
    while rest > 0:
        free = [i for i in range(amount - 1) if holding[i] < most]
        mass, remaining = sum([portions[i] for i in free]), rest
        for i in free:
            more = min(most - holding[i], max(1, remaining * portions[i] // mass), rest)
            holding[i] = holding[i] + more
            rest = rest - more
    return np.array([most] + holding)


def uneven_parts(stream_key, count, total, bound, skew):
    if count == 2:
        one = jax.random.randint(stream_key, (), max(1, total - bound), min(bound, total - 1) + 1)
        return jnp.stack([one, total - one])
    sizes = jnp.asarray(profile(count, total, bound, skew), jnp.int32)
    couples = (count - 1) // 2
    donor, receiver = sizes[1:1 + 2 * couples:2], sizes[2:2 + 2 * couples:2]
    margin = jnp.minimum(donor - 1, bound - receiver)
    shifted = jax.random.randint(jax.random.fold_in(stream_key, 1), (couples,), 0, 1 << 20) % (margin + 1)
    sizes = sizes.at[1:1 + 2 * couples:2].set(donor - shifted).at[2:2 + 2 * couples:2].set(receiver + shifted)
    return sizes[jax.random.permutation(jax.random.fold_in(stream_key, 2), count)]


def centred(stream_key, extent, scale, limit, shards=(), held_as=jnp.bfloat16):
    values = scale * jax.random.normal(stream_key, extent, jnp.float32)
    if shards:
        values = values * levels(stream_key, extent, shards, -0.22, 0.18)
    return jnp.clip(values, -limit, limit).astype(held_as)


def setup_inputs(seed: int = 0) -> dict:
    seeds = jax.random.split(jax.random.key(seed), 15)
    return {
        "inputs": centred(seeds[0], (MICRO, SEQUENCES, SEQ_LEN, D), 1.0, 6.0, ((1, 16), (2, 2))),
        "lengths": jax.vmap(lambda own: uneven_parts(own, SEQUENCES, VALID, SEQ_LEN, 0))(jax.random.split(seeds[1], MICRO)).reshape((MICRO, SEQUENCES)).astype(jnp.int32),
        "cotangent": centred(seeds[2], (MICRO, SEQUENCES, SEQ_LEN, D), 1.0, 6.0, ((1, 16), (2, 2))),
        "feed_in": centred(seeds[3], (2, D, FF), D ** -0.5, 0.375, ((2, 32),)),
        "feed_in_bias": centred(seeds[4], (2, FF), 0.5, 3.0, ((1, 32),)),
        "feed_out": centred(seeds[5], (2, FF, D), (FF // 4) ** -0.5, 0.375, ((1, 32),)),
        "attend_in": centred(seeds[6], (4, D, D), D ** -0.5, 0.375, ((2, 32),)),
        "attend_out": centred(seeds[7], (D, D), (D // 16) ** -0.5, 1.5, ((1, 32),)),
        "point_in": centred(seeds[8], (D, 2 * D), D ** -0.5, 0.375, ((1, 32),)),
        "point_in_bias": centred(seeds[9], (2 * D,), 0.5, 3.0, ((0, 32),)),
        "depth_kernel": centred(seeds[10], (KERNEL, D), KERNEL ** -0.5, 1.0, ((1, 32),)),
        "point_out": centred(seeds[11], (D, D), (D // 2) ** -0.5, 0.5, ((1, 32),)),
        "gains": jnp.clip(1.0 + 0.15 * jax.random.normal(seeds[12], (6, D), jnp.float32), 0.25, 1.75).astype(jnp.bfloat16),
        "biases": centred(seeds[13], (14, D), 0.3, 3.0, ((1, 32),)),
    }


@jax.custom_vjp
def low(v):
    return lax.optimization_barrier(v.astype(jnp.bfloat16)).astype(jnp.float32)

@jax.custom_vjp
def low_back(v):
    return v

def low_keep(v):
    return (low(v), None)

def low_pass(kept, grad):
    return (grad,)

def back_keep(v):
    return (v, None)

def back_low(kept, grad):
    return (low(grad),)
low.defvjp(low_keep, low_pass)
low_back.defvjp(back_keep, back_low)
EPSILON = 1e-05
HIGHEST = lax.Precision.HIGHEST
MASKED = -1000000000.0

def layer_norm(value, gain, shift):
    center = lax.optimization_barrier(jnp.mean(value, -1, keepdims=True))
    spread = value - center
    variance = lax.optimization_barrier(jnp.mean(spread * spread, -1, keepdims=True))
    return spread * lax.rsqrt(variance + EPSILON) * gain + shift

def product(left, right):
    return low_back(jnp.dot(left, right, precision=HIGHEST))

def sinusoid(offsets, width):
    frequency = jnp.exp(jnp.arange(width // 2, dtype=jnp.float32) * (-2.0 * math.log(10000.0) / width))
    angles = offsets.astype(jnp.float32)[:, None] * frequency[None, :]
    return jnp.concatenate([jnp.sin(angles), jnp.cos(angles)], axis=1)

def relative_shift(scores, count):
    row_count = scores.shape[-2]
    span = scores.shape[-1]
    leading = scores.shape[:-2]
    flipped = jnp.flip(scores, -1).reshape(leading + (row_count * span,))
    picked = lax.slice_in_dim(flipped, row_count - 1, row_count - 1 + row_count * (span - 1), axis=len(leading))
    return picked.reshape(leading + (row_count, span - 1))[..., :count]

def attend(query_content, query_position, keys, values, length, position_rows):
    key_count = keys.shape[0]
    scale = keys.shape[-1] ** (-0.5)
    content = jnp.einsum('ahe,jhe->haj', query_content, keys, precision=HIGHEST)
    position = jnp.einsum('ahe,rhe->har', query_position, position_rows, precision=HIGHEST)
    scores = low_back((content + relative_shift(position, key_count)) * scale)
    valid = jnp.arange(key_count, dtype=jnp.int32) < length
    masked = jnp.where(valid[None, None, :], scores, MASKED)
    peak = lax.optimization_barrier(jnp.max(masked, -1, keepdims=True))
    raised = jnp.exp(masked - peak)
    weights = raised / lax.optimization_barrier(jnp.sum(raised, -1, keepdims=True))
    return low_back(jnp.einsum('haj,jhe->ahe', low(weights), values, precision=HIGHEST))

def conformer(lengths, value, feed_in, feed_in_bias, feed_out, attend_in, attend_out, point_in, point_in_bias, depth_kernel, point_out, gains, biases):
    seq_count, seq_len, width = value.shape
    head_count = width // HEAD

    def feed(current, index):
        normed = low(layer_norm(current, gains[3 * index], biases[3 * index]))
        hidden = product(normed, feed_in[index]) + feed_in_bias[index]
        gated = low(jax.nn.silu(hidden))
        return current + 0.5 * (product(gated, feed_out[index]) + biases[5 + index])
    first_value = feed(value, 0)
    normed = low(layer_norm(first_value, gains[1], biases[1]))
    query = product(normed, attend_in[0]) + biases[7]
    keys = low(product(normed, attend_in[1]))
    values = low(product(normed, attend_in[2]) + biases[8])
    heads_shape = (seq_count, seq_len, head_count, HEAD)
    query_content = low(query + biases[10]).reshape(heads_shape)
    query_position = low(query + biases[11]).reshape(heads_shape)
    offsets = jnp.arange(2 * seq_len - 1, dtype=jnp.int32) - (seq_len - 1)
    table = low(sinusoid(offsets, width))
    position_rows = low(jnp.dot(table, attend_in[3], precision=HIGHEST)).reshape(2 * seq_len - 1, head_count, HEAD)
    checked = jax.checkpoint(attend)
    mixed = lax.map(lambda item: checked(item[0], item[1], item[2], item[3], item[4], position_rows), (query_content, query_position, keys.reshape(heads_shape), values.reshape(heads_shape), lengths))
    second_value = first_value + product(low(mixed.reshape(seq_count, seq_len, width)), attend_out) + biases[9]
    normed = low(layer_norm(second_value, gains[2], biases[2]))
    joint = product(normed, point_in) + point_in_bias
    valid = (jnp.arange(seq_len, dtype=jnp.int32)[None, :] < lengths[:, None]).astype(jnp.float32)[:, :, None]
    gated = low(joint[..., :width] * jax.nn.sigmoid(joint[..., width:]) * valid)
    half = depth_kernel.shape[0] // 2
    padded = jnp.pad(gated, ((0, 0), (half, half), (0, 0)))
    filtered = padded[:, 0:seq_len, :] * depth_kernel[0]
    for offset in range(1, depth_kernel.shape[0]):
        filtered = filtered + padded[:, offset:offset + seq_len, :] * depth_kernel[offset]
    filtered = low_back(filtered)
    center = lax.optimization_barrier(jnp.sum(filtered * valid, (0, 1))) / VALID
    spread = (filtered - center) * valid
    variance = lax.optimization_barrier(jnp.sum(spread * spread, (0, 1))) / VALID
    standard = (filtered - center) * lax.rsqrt(variance + EPSILON)
    swished = low(jax.nn.silu(standard * gains[5] + biases[13]))
    third_value = second_value + product(swished, point_out) + biases[12]
    fourth_value = feed(third_value, 1)
    return layer_norm(fourth_value, gains[4], biases[4])

def reference(inputs, lengths, cotangent, feed_in, feed_in_bias, feed_out, attend_in, attend_out, point_in, point_in_bias, depth_kernel, point_out, gains, biases):
    weights = tuple((array.astype(jnp.float32) for array in (feed_in, feed_in_bias, feed_out, attend_in, attend_out, point_in, point_in_bias, depth_kernel, point_out, gains, biases)))
    outs_list = []
    grads_list = []
    totals = None
    for micro in range(inputs.shape[0]):
        result, pullback = jax.vjp(partial(conformer, lengths[micro]), inputs[micro].astype(jnp.float32), *weights)
        pieces = pullback(cotangent[micro].astype(jnp.float32))
        outs_list.append(result.astype(jnp.bfloat16))
        grads_list.append(pieces[0])
        if totals is None:
            totals = pieces[1:]
        else:
            totals = tuple((earlier + later for earlier, later in zip(totals, pieces[1:])))
    return (jnp.stack(outs_list), jnp.stack(grads_list), totals[0], totals[1], totals[2], totals[3], totals[4], totals[5], totals[6], totals[7], totals[8], totals[9], totals[10])
```

```python
import math
from functools import partial

import jax
import jax.numpy as jnp
from jax import lax
from jax.experimental import pallas as pl
from jax.experimental.pallas import tpu as pltpu
from jax.sharding import PartitionSpec as P

HEAD = 64


EPSILON = 1e-05
HIGHEST = lax.Precision.HIGHEST
MASKED = -1000000000.0


def with_halo(cells, sides, width):
    for axis, dim in sides:
        count = lax.axis_size(axis)
        ends = count - 1
        head = lax.slice_in_dim(cells, 0, width, axis=dim)
        tail = lax.slice_in_dim(cells, cells.shape[dim] - width, cells.shape[dim], axis=dim)
        cells = jnp.concatenate(
            [
                lax.ppermute(tail, axis, [(i, (i + 1) % count) for i in range(ends)]),
                cells,
                lax.ppermute(head, axis, [((i + 1) % count, i) for i in range(ends)]),
            ],
            axis=dim,
        )
    return cells


def layer_norm(value, gain, shift):
    center = jnp.mean(value, -1, keepdims=True)
    spread = value - center
    variance = jnp.mean(spread * spread, -1, keepdims=True)
    return spread * lax.rsqrt(variance + EPSILON) * gain + shift


def norm_backward(gradient, value, gain, shift):
    pull = jax.vjp(layer_norm, value, gain, shift)[1]
    return pull(gradient)


def sinusoid(offsets, width):
    frequency = jnp.exp(
        jnp.arange(width // 2, dtype=jnp.float32) * (-2.0 * math.log(10000.0) / width)
    )
    angles = offsets.astype(jnp.float32)[:, None] * frequency[None, :]
    return jnp.concatenate([jnp.sin(angles), jnp.cos(angles)], axis=1)


def relative_shift(scores, count):
    row_count = scores.shape[-2]
    span = scores.shape[-1]
    leading = scores.shape[:-2]
    flipped = jnp.flip(scores, -1).reshape(leading + (row_count * span,))
    picked = lax.slice_in_dim(
        flipped, row_count - 1, row_count - 1 + row_count * (span - 1), axis=len(leading)
    )
    return picked.reshape(leading + (row_count, span - 1))[..., :count]


def relative_unshift(gradient, span):
    row_count = gradient.shape[-2]
    count = gradient.shape[-1]
    leading = gradient.shape[:-2]
    widened = jnp.pad(gradient, [(0, 0)] * len(leading) + [(0, 0), (0, span - 1 - count)])
    flat = widened.reshape(leading + (row_count * (span - 1),))
    placed = jnp.pad(flat, [(0, 0)] * len(leading) + [(row_count - 1, 1)])
    return jnp.flip(placed.reshape(leading + (row_count, span)), -1)


def matmul(left, right):
    return jnp.dot(left, right, preferred_element_type=jnp.float32)


def matmul_back(left, right):
    return lax.dot_general(
        left, right, (((1,), (1,)), ((), ())), preferred_element_type=jnp.float32
    )


def outer_sum(left, right):
    return lax.dot_general(
        left, right, (((0,), (0,)), ((), ())), preferred_element_type=jnp.float32
    )


def gate_linear(joint):
    width = joint.shape[1] // 2
    return joint[:, :width] * jax.nn.sigmoid(joint[:, width:])


def fetch_forward(local):
    return (
        lax.all_gather(local[0], ("dp", "seq"), axis=2, tiled=True),
        lax.all_gather(local[1], ("dp", "seq"), axis=1, tiled=True),
        lax.all_gather(local[2], ("dp", "seq"), axis=1, tiled=True),
        lax.all_gather(local[3], ("dp", "seq"), axis=2, tiled=True),
        lax.all_gather(local[4], ("dp", "seq"), axis=1, tiled=True),
        lax.all_gather(local[5], ("dp", "seq"), axis=1, tiled=True),
        lax.all_gather(local[6], ("dp", "seq"), axis=0, tiled=True),
        lax.all_gather(local[7], ("dp", "seq"), axis=1, tiled=True),
        lax.all_gather(local[8], ("dp", "seq"), axis=1, tiled=True),
        lax.all_gather(local[9], ("dp", "seq"), axis=1, tiled=True),
        lax.all_gather(local[10], ("dp", "seq"), axis=1, tiled=True),
    )


def fetch_backward(local):
    return (
        lax.all_gather(local[0], ("dp", "seq"), axis=2, tiled=True),
        lax.all_gather(local[1], ("dp", "seq"), axis=1, tiled=True),
        lax.all_gather(local[2], ("dp", "seq"), axis=1, tiled=True),
        lax.all_gather(local[3], ("dp", "seq"), axis=2, tiled=True),
        lax.all_gather(local[4], ("dp", "seq"), axis=1, tiled=True),
        lax.all_gather(local[5], ("dp", "seq"), axis=1, tiled=True),
        lax.all_gather(local[6], ("dp", "seq"), axis=0, tiled=True),
        lax.all_gather(local[7], ("dp", "seq"), axis=1, tiled=True),
        lax.all_gather(local[8], ("dp", "seq"), axis=1, tiled=True),
        lax.all_gather(local[9], ("dp", "seq"), axis=1, tiled=True),
        lax.all_gather(local[10], ("dp", "seq"), axis=1, tiled=True),
    )


def sum_at_end(totals):
    return (
        lax.psum_scatter(totals[0], ("dp", "seq"), scatter_dimension=2, tiled=True),
        lax.psum_scatter(totals[1], ("dp", "seq"), scatter_dimension=1, tiled=True),
        lax.psum_scatter(totals[2], ("dp", "seq"), scatter_dimension=1, tiled=True),
        lax.psum_scatter(totals[3], ("dp", "seq"), scatter_dimension=2, tiled=True),
        lax.psum_scatter(totals[4], ("dp", "seq"), scatter_dimension=1, tiled=True),
        lax.psum_scatter(totals[5], ("dp", "seq"), scatter_dimension=1, tiled=True),
        lax.psum_scatter(totals[6], ("dp", "seq"), scatter_dimension=0, tiled=True),
        lax.psum_scatter(totals[7], ("dp", "seq"), scatter_dimension=1, tiled=True),
        lax.psum_scatter(totals[8], ("dp", "seq"), scatter_dimension=1, tiled=True),
        lax.psum_scatter(totals[9], ("dp", "seq"), scatter_dimension=1, tiled=True),
        lax.psum_scatter(totals[10], ("dp", "seq"), scatter_dimension=1, tiled=True),
    )


def feed_forward(value, whole, gains_wide, biases_wide, index):
    normed_low = layer_norm(value, gains_wide[3 * index], biases_wide[3 * index]).astype(
        jnp.bfloat16
    )
    hidden = matmul(normed_low, whole[0][index]) + whole[1][index].astype(jnp.float32)
    gated_low = jax.nn.silu(hidden).astype(jnp.bfloat16)
    branch = matmul(gated_low, whole[2][index]) + biases_wide[5 + index]
    return (value + 0.5 * branch, (value, normed_low, hidden, gated_low))


def feed_backward(gradient, kept, whole, gains_wide, biases_wide, index, totals):
    value, normed_low, hidden, gated_low = kept
    branch_grad = 0.5 * gradient
    branch_low = branch_grad.astype(jnp.bfloat16)
    totals[10] = totals[10].at[5 + index].add(jnp.sum(branch_grad, 0))
    totals[2] = totals[2].at[index].add(outer_sum(gated_low, branch_low))
    gated_grad = matmul_back(branch_low, whole[2][index])
    hidden_grad = jax.vjp(jax.nn.silu, hidden)[1](gated_grad)[0]
    hidden_low = hidden_grad.astype(jnp.bfloat16)
    totals[1] = totals[1].at[index].add(jnp.sum(hidden_grad, 0))
    totals[0] = totals[0].at[index].add(outer_sum(normed_low, hidden_low))
    normed_grad = matmul_back(hidden_low, whole[0][index])
    value_grad, gain_grad, shift_grad = norm_backward(
        normed_grad, value, gains_wide[3 * index], biases_wide[3 * index]
    )
    totals[9] = totals[9].at[3 * index].add(gain_grad)
    totals[10] = totals[10].at[3 * index].add(shift_grad)
    return gradient + value_grad


def score_table(query_content, query_position, keys_all, position_rows):
    seq_count, key_count, width = keys_all.shape
    head_count = position_rows.shape[1]
    head_size = position_rows.shape[2]
    keys_heads = keys_all.reshape(seq_count, key_count, head_count, head_size)
    content = jnp.einsum(
        "sahe,sjhe->shaj", query_content, keys_heads, preferred_element_type=jnp.float32
    )
    position = jnp.einsum(
        "sahe,rhe->shar", query_position, position_rows, preferred_element_type=jnp.float32
    )
    return (content + relative_shift(position, key_count)) * head_size ** (-0.5)


def attention_forward(value, whole, gains_wide, biases_wide, valid_keys, table_low, seq_count):
    row_count, width = value.shape
    tok_count = row_count // seq_count
    head_count = width // HEAD
    heads_shape = (seq_count, tok_count, head_count, HEAD)
    normed_low = layer_norm(value, gains_wide[1], biases_wide[1]).astype(jnp.bfloat16)
    query = matmul(normed_low, whole[3][0]) + biases_wide[7]
    keys_low = (
        matmul(normed_low, whole[3][1]).astype(jnp.bfloat16).reshape(seq_count, tok_count, width)
    )
    values_low = (
        (matmul(normed_low, whole[3][2]) + biases_wide[8])
        .astype(jnp.bfloat16)
        .reshape(seq_count, tok_count, width)
    )
    query_content = (query + biases_wide[10]).astype(jnp.bfloat16).reshape(heads_shape)
    query_position = (query + biases_wide[11]).astype(jnp.bfloat16).reshape(heads_shape)
    position_rows = (
        matmul(table_low, whole[3][3]).astype(jnp.bfloat16).reshape(-1, head_count, HEAD)
    )
    keys_all, values_all = (
        lax.all_gather(keys_low, "seq", axis=1, tiled=True),
        lax.all_gather(values_low, "seq", axis=1, tiled=True),
    )
    scores = score_table(query_content, query_position, keys_all, position_rows)
    masked = jnp.where(valid_keys, scores, MASKED)
    peak = jnp.max(masked, -1, keepdims=True)
    raised = jnp.exp(masked - peak)
    total = jnp.sum(raised, -1, keepdims=True)
    probs_low = (raised / total).astype(jnp.bfloat16)
    log_total = peak + jnp.log(total)
    values_heads = values_all.reshape(seq_count, -1, head_count, HEAD)
    mixed = jnp.einsum(
        "shaj,sjhe->sahe", probs_low, values_heads, preferred_element_type=jnp.float32
    )
    mixed_low = mixed.astype(jnp.bfloat16).reshape(row_count, width)
    branch = matmul(mixed_low, whole[4]) + biases_wide[9]
    kept = (
        value,
        normed_low,
        query_content,
        query_position,
        keys_all,
        values_all,
        position_rows,
        log_total,
        mixed_low,
    )
    return (value + branch, kept)


def attention_backward(
    gradient, kept, whole, gains_wide, biases_wide, valid_keys, table_low, totals
):
    (
        value,
        normed_low,
        query_content,
        query_position,
        keys_all,
        values_all,
        position_rows,
        log_total,
        mixed_low,
    ) = kept
    seq_count, tok_count, head_count, head_size = query_content.shape
    key_count = keys_all.shape[1]
    row_count, width = value.shape
    scale = head_size ** (-0.5)
    gradient_low = gradient.astype(jnp.bfloat16)
    totals[10] = totals[10].at[9].add(jnp.sum(gradient, 0))
    totals[4] = totals[4] + outer_sum(mixed_low, gradient_low)
    mixed_grad = (
        matmul_back(gradient_low, whole[4])
        .astype(jnp.bfloat16)
        .reshape(seq_count, tok_count, head_count, head_size)
    )
    scores = score_table(query_content, query_position, keys_all, position_rows)
    probs = jnp.where(valid_keys, jnp.exp(scores - log_total), 0.0)
    values_heads = values_all.reshape(seq_count, key_count, head_count, head_size)
    keys_heads = keys_all.reshape(seq_count, key_count, head_count, head_size)
    values_grad = jnp.einsum(
        "shaj,sahe->sjhe",
        probs.astype(jnp.bfloat16),
        mixed_grad,
        preferred_element_type=jnp.float32,
    )
    probs_grad = jnp.einsum(
        "sahe,sjhe->shaj", mixed_grad, values_heads, preferred_element_type=jnp.float32
    )
    score_grad = probs * (probs_grad - jnp.sum(probs_grad * probs, -1, keepdims=True))
    score_low = score_grad.astype(jnp.bfloat16)
    content_grad = (
        jnp.einsum("shaj,sjhe->sahe", score_low, keys_heads, preferred_element_type=jnp.float32)
        * scale
    )
    keys_grad = (
        jnp.einsum("shaj,sahe->sjhe", score_low, query_content, preferred_element_type=jnp.float32)
        * scale
    )
    position_low = relative_unshift(score_low, position_rows.shape[0])
    offset_grad = (
        jnp.einsum(
            "shar,rhe->sahe", position_low, position_rows, preferred_element_type=jnp.float32
        )
        * scale
    )
    rows_grad = (
        jnp.einsum(
            "shar,sahe->rhe", position_low, query_position, preferred_element_type=jnp.float32
        )
        * scale
    )
    table_wide = table_low.astype(jnp.float32)
    totals[3] = (
        totals[3]
        .at[3]
        .add(
            lax.dot_general(
                table_wide,
                rows_grad.reshape(-1, width),
                (((0,), (0,)), ((), ())),
                precision=HIGHEST,
            )
        )
    )
    keys_sum, values_sum = (
        lax.psum_scatter(
            keys_grad.reshape(seq_count, key_count, width).astype(jnp.bfloat16),
            "seq",
            scatter_dimension=1,
            tiled=True,
        ).astype(jnp.float32),
        lax.psum_scatter(
            values_grad.reshape(seq_count, key_count, width).astype(jnp.bfloat16),
            "seq",
            scatter_dimension=1,
            tiled=True,
        ).astype(jnp.float32),
    )
    keys_sum = keys_sum.reshape(row_count, width)
    values_sum = values_sum.reshape(row_count, width)
    content_flat = content_grad.reshape(row_count, width)
    offset_flat = offset_grad.reshape(row_count, width)
    query_grad = content_flat + offset_flat
    totals[10] = totals[10].at[7].add(jnp.sum(query_grad, 0)).at[8].add(jnp.sum(values_sum, 0))
    totals[10] = totals[10].at[10].add(jnp.sum(content_flat, 0)).at[11].add(jnp.sum(offset_flat, 0))
    query_low = query_grad.astype(jnp.bfloat16)
    keys_low = keys_sum.astype(jnp.bfloat16)
    values_low = values_sum.astype(jnp.bfloat16)
    totals[3] = (
        totals[3]
        .at[0]
        .add(outer_sum(normed_low, query_low))
        .at[1]
        .add(outer_sum(normed_low, keys_low))
        .at[2]
        .add(outer_sum(normed_low, values_low))
    )
    normed_grad = (
        matmul_back(query_low, whole[3][0])
        + matmul_back(keys_low, whole[3][1])
        + matmul_back(values_low, whole[3][2])
    )
    value_grad, gain_grad, shift_grad = norm_backward(
        normed_grad, value, gains_wide[1], biases_wide[1]
    )
    totals[9] = totals[9].at[1].add(gain_grad)
    totals[10] = totals[10].at[1].add(shift_grad)
    return gradient + value_grad


def convolution_forward(value, whole, gains_wide, biases_wide, valid, valid_total, seq_count):
    row_count, width = value.shape
    tok_count = row_count // seq_count
    kernel_size = whole[7].shape[0]
    half = kernel_size // 2
    normed_low = layer_norm(value, gains_wide[2], biases_wide[2]).astype(jnp.bfloat16)
    joint = matmul(normed_low, whole[5]) + whole[6].astype(jnp.float32)
    gated_low = (gate_linear(joint).reshape(seq_count, tok_count, width) * valid).astype(
        jnp.bfloat16
    )
    extended = with_halo(gated_low, (("seq", 1),), half)
    extended_wide = extended.astype(jnp.float32)
    kernel = whole[7].astype(jnp.float32)
    filtered = extended_wide[:, 0:tok_count, :] * kernel[0]
    for offset in range(1, kernel_size):
        filtered = filtered + extended_wide[:, offset : offset + tok_count, :] * kernel[offset]
    center = lax.psum(jnp.sum(filtered * valid, (0, 1)), ("dp", "seq")) / valid_total
    spread = (filtered - center) * valid
    variance = lax.psum(jnp.sum(spread * spread, (0, 1)), ("dp", "seq")) / valid_total
    reciprocal = lax.rsqrt(variance + EPSILON)
    standard = (filtered - center) * reciprocal
    shaped = standard * gains_wide[5] + biases_wide[13]
    swished_low = jax.nn.silu(shaped).astype(jnp.bfloat16).reshape(row_count, width)
    branch = matmul(swished_low, whole[8]) + biases_wide[12]
    return (
        value + branch,
        (value, normed_low, joint, extended, standard, reciprocal, shaped, swished_low),
    )


def convolution_backward(
    gradient, kept, whole, gains_wide, biases_wide, valid, valid_total, totals
):
    value, normed_low, joint, extended, standard, reciprocal, shaped, swished_low = kept
    seq_count, tok_count, width = standard.shape
    row_count = seq_count * tok_count
    kernel_size = whole[7].shape[0]
    half = kernel_size // 2
    gradient_low = gradient.astype(jnp.bfloat16)
    totals[10] = totals[10].at[12].add(jnp.sum(gradient, 0))
    totals[8] = totals[8] + outer_sum(swished_low, gradient_low)
    swished_grad = matmul_back(gradient_low, whole[8]).reshape(seq_count, tok_count, width)
    shaped_grad = jax.vjp(jax.nn.silu, shaped)[1](swished_grad)[0]
    beta_local = jnp.sum(shaped_grad, (0, 1))
    gamma_local = jnp.sum(shaped_grad * standard, (0, 1))
    totals[9] = totals[9].at[5].add(gamma_local)
    totals[10] = totals[10].at[13].add(beta_local)
    beta_all, gamma_all = lax.psum((beta_local, gamma_local), ("dp", "seq"))
    filtered_grad = (
        reciprocal
        * gains_wide[5]
        * (shaped_grad - valid * (beta_all + standard * gamma_all) / valid_total)
    )
    filtered_low = filtered_grad.astype(jnp.bfloat16)
    extended_wide = extended.astype(jnp.float32)
    filtered_wide = filtered_low.astype(jnp.float32)
    kernel_grad = jnp.stack(
        [
            jnp.sum(extended_wide[:, offset : offset + tok_count, :] * filtered_wide, (0, 1))
            for offset in range(kernel_size)
        ]
    )
    totals[7] = totals[7] + kernel_grad
    rim = with_halo(filtered_low, (("seq", 1),), half)
    rim_wide = rim.astype(jnp.float32)
    kernel = whole[7].astype(jnp.float32)
    gated_grad = rim_wide[:, 2 * half : 2 * half + tok_count, :] * kernel[0]
    for offset in range(1, kernel_size):
        gated_grad = (
            gated_grad
            + rim_wide[:, 2 * half - offset : 2 * half - offset + tok_count, :] * kernel[offset]
        )
    glu_grad = (gated_grad * valid).reshape(row_count, width)
    joint_grad = jax.vjp(gate_linear, joint)[1](glu_grad)[0]
    joint_low = joint_grad.astype(jnp.bfloat16)
    totals[6] = totals[6] + jnp.sum(joint_grad, 0)
    totals[5] = totals[5] + outer_sum(normed_low, joint_low)
    normed_grad = matmul_back(joint_low, whole[5])
    value_grad, gain_grad, shift_grad = norm_backward(
        normed_grad, value, gains_wide[2], biases_wide[2]
    )
    totals[9] = totals[9].at[2].add(gain_grad)
    totals[10] = totals[10].at[2].add(shift_grad)
    return gradient + value_grad


def body(
    inputs,
    lengths,
    cotangent,
    feed_in,
    feed_in_bias,
    feed_out,
    attend_in,
    attend_out,
    point_in,
    point_in_bias,
    depth_kernel,
    point_out,
    gains,
    biases,
):
    local = (
        feed_in,
        feed_in_bias,
        feed_out,
        attend_in,
        attend_out,
        point_in,
        point_in_bias,
        depth_kernel,
        point_out,
        gains,
        biases,
    )
    micro_count, seq_count, tok_count, width = inputs.shape
    seq_len = tok_count * lax.axis_size("seq")
    valid_total = seq_count * lax.axis_size("dp") * seq_len * 3 // 4
    first = lax.axis_index("seq") * tok_count
    positions = first + jnp.arange(tok_count, dtype=jnp.int32)
    offsets = first - seq_len + 1 + jnp.arange(seq_len + tok_count - 1, dtype=jnp.int32)
    table_low = sinusoid(offsets, width).astype(jnp.bfloat16)
    key_places = jnp.arange(seq_len, dtype=jnp.int32)
    layer_outs = []
    input_grads = []
    totals = None
    shards = None
    for micro in range(micro_count):
        whole = fetch_forward(local)
        if totals is None:
            totals = [jnp.zeros(array.shape, jnp.float32) for array in whole]
        gains_wide = whole[9].astype(jnp.float32)
        biases_wide = whole[10].astype(jnp.float32)
        lengths_now = lengths[micro]
        valid = (positions[None, :] < lengths_now[:, None]).astype(jnp.float32)[:, :, None]
        valid_keys = (key_places[None, :] < lengths_now[:, None])[:, None, None, :]
        start_value = inputs[micro].astype(jnp.float32).reshape(seq_count * tok_count, width)
        first_value, first_kept = feed_forward(start_value, whole, gains_wide, biases_wide, 0)
        second_value, second_kept = attention_forward(
            first_value, whole, gains_wide, biases_wide, valid_keys, table_low, seq_count
        )
        third_value, third_kept = convolution_forward(
            second_value, whole, gains_wide, biases_wide, valid, valid_total, seq_count
        )
        fourth_value, fourth_kept = feed_forward(third_value, whole, gains_wide, biases_wide, 1)
        final = layer_norm(fourth_value, gains_wide[4], biases_wide[4])
        layer_outs.append(final.astype(jnp.bfloat16).reshape(seq_count, tok_count, width))
        whole = fetch_backward(local)
        gradient = cotangent[micro].astype(jnp.float32).reshape(seq_count * tok_count, width)
        gradient, gain_grad, shift_grad = norm_backward(
            gradient, fourth_value, gains_wide[4], biases_wide[4]
        )
        totals[9] = totals[9].at[4].add(gain_grad)
        totals[10] = totals[10].at[4].add(shift_grad)
        gradient = feed_backward(gradient, fourth_kept, whole, gains_wide, biases_wide, 1, totals)
        gradient = convolution_backward(
            gradient, third_kept, whole, gains_wide, biases_wide, valid, valid_total, totals
        )
        gradient = attention_backward(
            gradient, second_kept, whole, gains_wide, biases_wide, valid_keys, table_low, totals
        )
        gradient = feed_backward(gradient, first_kept, whole, gains_wide, biases_wide, 0, totals)
        input_grads.append(gradient.reshape(seq_count, tok_count, width))
    shards = sum_at_end(totals)
    return (
        jnp.stack(layer_outs),
        jnp.stack(input_grads),
        shards[0],
        shards[1],
        shards[2],
        shards[3],
        shards[4],
        shards[5],
        shards[6],
        shards[7],
        shards[8],
        shards[9],
        shards[10],
    )

LOW = jnp.bfloat16
WIDE = jnp.float32
BLOCK = 256
AXIS_BITS = (("seq", 1), ("dp", 1), ("dp", 2), ("dp", 4), ("dp", 8))
ORDER_A = (4, 3, 2, 0, 1)
ORDER_B = (0, 4, 3, 2, 1)
ORDER_C = (2, 0, 4, 3, 1)
EDGE = 16
CONV_ROWS = 64


def swap(value, axis, bit):
    return lax.ppermute(value, axis, [(i, i ^ bit) for i in range(lax.axis_size(axis))])


def gather_chain(block, order):
    held = block[None]
    for which in order:
        held = jnp.concatenate([held, swap(held, *AXIS_BITS[which])], 0)
    return held


def scatter_chain(held, order):
    for which in reversed(order):
        half = held.shape[0] // 2
        arrived = swap(held[half:], *AXIS_BITS[which])
        total = held[:half].astype(WIDE) + arrived.astype(WIDE)
        held = total if half == 1 else total.astype(LOW)
    return held[0]


def place(mask, order):
    return sum(((mask >> which) & 1) << at for at, which in enumerate(order))


def nn(a, b):
    return lax.dot_general(a, b, (((1,), (0,)), ((), ())), preferred_element_type=WIDE)


def nt(a, b):
    return lax.dot_general(a, b, (((1,), (1,)), ((), ())), preferred_element_type=WIDE)


def tn(a, b):
    return lax.dot_general(a, b, (((0,), (0,)), ((), ())), preferred_element_type=WIDE)


def normed(value):
    center = jnp.mean(value, -1, keepdims=True)
    spread = value - center
    rate = lax.rsqrt(jnp.mean(spread * spread, -1, keepdims=True) + EPSILON)
    return spread * rate, rate


def normed_back(gradient, unit, rate, gain):
    inner = gradient * gain
    mean_one = jnp.mean(inner, -1, keepdims=True)
    mean_two = jnp.mean(inner * unit, -1, keepdims=True)
    return (inner - mean_one - unit * mean_two) * rate


def column_sum(value):
    return jnp.sum(value, 0, keepdims=True)


def sigmoid(value):
    return 1.0 / (1.0 + jnp.exp(-value))


def rows_at(at, size):
    return pl.ds(pl.multiple_of(at * size, size), size)


def row_numbers(first, size):
    return first + lax.broadcasted_iota(jnp.int32, (size, 1), 0)


def windows(padded, first, size):
    window = padded[pl.ds(pl.multiple_of(first, size), size + 32), :]
    for residue in range(8):
        moved = window[residue : residue + size + 24, :]
        for step in range(4):
            offset = 8 * step + residue
            if offset:
                yield offset, moved[8 * step : 8 * step + size, :]


def gain_row(small, at):
    return small[at : at + 1, :]


def bias_row(small, at):
    return small[6 + at : 7 + at, :]


def tap_row(small, at):
    return small[20 + at : 21 + at, :]


def prep_kernel(meta, ga, gb, wat, wao, wpi, wpo, small, fb, pb, wide, wide_pi, turned):
    own_a, own_b = meta[2], meta[3]
    for r in range(32):
        block = gb[own_b ^ place(r, ORDER_B)].astype(WIDE)
        rows = slice(8 * r, 8 * r + 8)
        for k in range(5):
            wide[k, rows, :] = block[8 * k : 8 * k + 8, :]
        wide_pi[16 * r : 16 * r + 16, :] = block[40:56, :]
        wide[5, rows, :] = block[56:64, :]
        extra = ga[own_a ^ place(r, ORDER_A), 64:80, :].astype(WIDE)
        turned[rows, :] = extra[0:8, 0:128]
        pb[0:1, 16 * r : 16 * r + 16] = extra[8:9, 64:80]
        extra = ga[place(r, ORDER_A), 64:80, :].astype(WIDE)
        a, c = 32 * place(r, ORDER_A), 32 * place(r, ORDER_C)
        fb[0:1, a : a + 32] = extra[8:9, 0:32]
        fb[1:2, c : c + 32] = extra[8:9, 32:64]
    for k in range(4):
        wat[k] = wide[k].astype(LOW)
    wao[...] = wide[4].astype(LOW)
    wpo[...] = wide[5].astype(LOW)
    wpi[...] = wide_pi[...].astype(LOW)
    small[...] = turned[...].T


def first_weights(ref):
    return ref[:, 0:32, :].reshape(-1, ref.shape[2]), ref[:, 32:64, :].reshape(-1, ref.shape[2])


def fill_whole(meta, own, other, whole):
    half = other.shape[0]
    side = meta[0]
    whole[pl.ds(pl.multiple_of(side * half, half), half), :] = own[side, 0].astype(WIDE)
    whole[pl.ds(pl.multiple_of((1 - side) * half, half), half), :] = other[...].astype(WIDE)


def rotated(query_position, weight, sine, cosine):
    lead = nn(query_position, weight)
    quarter = lead.shape[1] // 2
    first, second = lead[:, :quarter], lead[:, quarter:]
    return jnp.concatenate(
        [second * sine - first * cosine, first * sine + second * cosine], 1
    ).astype(LOW)


def head_scores(qkv, wat, table, table_low, rows, cols):
    eighth = HEAD ** (-0.5)
    quarter = table.shape[1] // 2
    content = (qkv[0, rows, cols].astype(WIDE) * eighth).astype(LOW)
    position = (qkv[1, rows, cols].astype(WIDE) * eighth).astype(LOW)
    turned = rotated(
        position, wat[3, cols, :], table[rows, :quarter], table[rows, quarter:]
    )
    return nt(content, qkv[2, :, cols]) + nt(turned, table_low[...])


def forward_kernel(
    meta, own, other, ga, wat, wao, wpi, small, fb, pb, table, table_low,
    x1, qkv, mixed, logs, x2, gated, filtered, stats, whole, padded,
):
    tokens, width = x1.shape
    length = meta[1]
    fill_whole(meta, own, other, whole)

    @pl.loop(0, tokens // BLOCK)
    def _(at):
        rows = rows_at(at, BLOCK)
        x = whole[rows, :]
        low = (normed(x)[0] * gain_row(small, 0) + bias_row(small, 0)).astype(LOW)
        w_in, w_out = first_weights(ga)
        hidden = nt(low, w_in) + fb[0:1, :]
        active = (hidden * sigmoid(hidden)).astype(LOW)
        value = x + 0.5 * (nn(active, w_out) + bias_row(small, 5))
        x1[rows, :] = value
        low = (normed(value)[0] * gain_row(small, 1) + bias_row(small, 1)).astype(LOW)
        query = nt(low, wat[0]) + bias_row(small, 7)
        qkv[0, rows, :] = (query + bias_row(small, 10)).astype(LOW)
        qkv[1, rows, :] = (query + bias_row(small, 11)).astype(LOW)
        qkv[2, rows, :] = nt(low, wat[1]).astype(LOW)
        qkv[3, rows, :] = (nt(low, wat[2]) + bias_row(small, 8)).astype(LOW)

    padded[0:EDGE, :] = jnp.zeros((EDGE, width), WIDE)
    padded[EDGE + tokens : 2 * EDGE + tokens, :] = jnp.zeros((EDGE, width), WIDE)

    @pl.loop(0, tokens // BLOCK)
    def _(at):
        rows = rows_at(at, BLOCK)
        open_keys = lax.broadcasted_iota(jnp.int32, (1, tokens), 1) < length
        lane = lax.broadcasted_iota(jnp.int32, (1, 128), 1)
        kept = jnp.zeros((BLOCK, 128), WIDE)
        for head in range(width // HEAD):
            cols = slice(head * HEAD, head * HEAD + HEAD)
            scores = head_scores(qkv, wat, table, table_low, rows, cols)
            scores = jnp.where(open_keys, scores, MASKED)
            peak = jnp.max(scores, -1, keepdims=True)
            raised = jnp.exp(scores - peak)
            total = jnp.sum(raised, -1, keepdims=True)
            low = (raised * (1.0 / total)).astype(LOW)
            mixed[rows, cols] = nn(low, qkv[3, :, cols]).astype(LOW)
            kept = jnp.where(lane == head, peak + jnp.log(total), kept)
        logs[rows, :] = kept
        value = x1[rows, :] + nt(mixed[rows, :], wao[...]) + bias_row(small, 9)
        x2[rows, :] = value
        low = (normed(value)[0] * gain_row(small, 2) + bias_row(small, 2)).astype(LOW)
        joint = nt(low, wpi[...]) + pb[...]
        valid = (row_numbers(at * BLOCK, BLOCK) < length).astype(WIDE)
        linear = (joint[:, :width] * sigmoid(joint[:, width:]) * valid).astype(LOW)
        gated[rows, :] = linear
        padded[pl.ds(pl.multiple_of(EDGE + at * BLOCK, 16), BLOCK), :] = linear.astype(WIDE)

    @pl.loop(0, tokens // CONV_ROWS)
    def _(at):
        total = jnp.zeros((CONV_ROWS, width), WIDE)
        for offset, piece in windows(padded, at * CONV_ROWS, CONV_ROWS):
            total = total + piece * tap_row(small, offset - 1)
        filtered[rows_at(at, CONV_ROWS), :] = total

    count = length.astype(WIDE)
    valid = (row_numbers(0, tokens) < length).astype(WIDE)
    total = column_sum(filtered[...] * valid)
    spread = (filtered[...] - total / count) * valid
    stats[0:1, :] = total
    stats[1:2, :] = column_sum(spread * spread)
    stats[2:3, :] = jnp.zeros((1, width), WIDE) + count


def middle_kernel(
    valid_total,
    meta, own, other, stats, filtered, x2, wpo, gc, small, fb,
    keep, send, gx3, shaped_grad, norm_stats, sums, hidden_sum, low_hidden, low_active,
    low_normed, low_branch, low_swished, low_third, betas, whole, final,
):
    tokens, width = x2.shape
    half = keep.shape[0]
    side = meta[0]
    fill_whole(meta, own, other, whole)
    count = stats[:, 2, :]
    center = column_sum(stats[:, 0, :]) / valid_total
    shift = stats[:, 0, :] / count - center
    variance = column_sum(stats[:, 1, :] + count * shift * shift) / valid_total
    rate5 = lax.rsqrt(variance + EPSILON)
    norm_stats[0:1, :] = center
    norm_stats[1:2, :] = rate5
    sums[...] = jnp.zeros(sums.shape, WIDE)
    hidden_sum[...] = jnp.zeros(hidden_sum.shape, WIDE)
    betas[...] = jnp.zeros(betas.shape, WIDE)

    @pl.loop(0, tokens // BLOCK)
    def _(at):
        rows = rows_at(at, BLOCK)
        standard = (filtered[rows, :] - norm_stats[0:1, :]) * norm_stats[1:2, :]
        shaped = standard * gain_row(small, 5) + bias_row(small, 13)
        open5 = sigmoid(shaped)
        swished = (shaped * open5).astype(LOW)
        low_swished[rows, :] = swished
        x3 = x2[rows, :] + nt(swished, wpo[...]) + bias_row(small, 12)
        unit3, rate3 = normed(x3)
        low3 = (unit3 * gain_row(small, 3) + bias_row(small, 3)).astype(LOW)
        low_normed[rows, :] = low3
        w_in, w_out = first_weights(gc)
        hidden = nt(low3, w_in) + fb[1:2, :]
        opened = sigmoid(hidden)
        active = (hidden * opened).astype(LOW)
        low_active[rows, :] = active
        x4 = x3 + 0.5 * (nn(active, w_out) + bias_row(small, 6))
        unit4, rate4 = normed(x4)
        final[rows, :] = unit4 * gain_row(small, 4) + bias_row(small, 4)
        gy = whole[rows, :]
        sums[0:1, :] += column_sum(gy * unit4)
        sums[1:2, :] += column_sum(gy)
        gx4 = normed_back(gy, unit4, rate4, gain_row(small, 4))
        branch = 0.5 * gx4
        sums[2:3, :] += column_sum(branch)
        low_b = branch.astype(LOW)
        low_branch[rows, :] = low_b
        hidden_grad = nt(low_b, w_out) * (opened * (1.0 + hidden * (1.0 - opened)))
        hidden_sum[...] += column_sum(hidden_grad)
        low_h = hidden_grad.astype(LOW)
        low_hidden[rows, :] = low_h
        gn = nn(low_h, w_in)
        sums[3:4, :] += column_sum(gn * unit3)
        sums[4:5, :] += column_sum(gn)
        g3 = gx4 + normed_back(gn, unit3, rate3, gain_row(small, 3))
        gx3[rows, :] = g3
        sums[5:6, :] += column_sum(g3)
        low_g = g3.astype(LOW)
        low_third[rows, :] = low_g
        gs = nn(low_g, wpo[...]) * (open5 * (1.0 + shaped * (1.0 - open5)))
        shaped_grad[rows, :] = gs
        betas[0:1, :] += column_sum(gs)
        betas[1:2, :] += column_sum(gs * standard)

    keep[...] = final[pl.ds(pl.multiple_of(side * half, half), half), :].astype(LOW)
    send[...] = final[pl.ds(pl.multiple_of((1 - side) * half, half), half), :].astype(LOW)


def outer_kernel(low_hidden, low_active, low_normed, low_branch, low_swished, low_third, out, wpo_grad):
    blocks, rows, width = out.shape
    out[:, 0:32, :] = tn(low_hidden[...], low_normed[...]).astype(LOW).reshape(blocks, 32, width)
    out[:, 32:64, :] = tn(low_active[...], low_branch[...]).astype(LOW).reshape(blocks, 32, width)
    wpo_grad[...] = tn(low_third[...], low_swished[...])


def back_kernel(
    valid_total,
    meta, betas, norm_stats, filtered, shaped_grad, gx3, gated, x2, x1, qkv, mixed, logs,
    table, table_low, wat, wao, wpi, small, pb, wpo_grad,
    gx1, out, sums, joint_sum,
    padded, padded_g, taps, gx2, low_a, mix_grad, query_c, query_p, key_g, value_g, w3_grad, wide, wide_pi,
):
    tokens, width = x1.shape
    length = meta[1]
    own_b = meta[3]
    heads = width // HEAD
    quarter = table.shape[1] // 2
    eighth = HEAD ** (-0.5)
    edge = jnp.zeros((EDGE, width), WIDE)
    for ref in (padded, padded_g):
        ref[0:EDGE, :] = edge
        ref[EDGE + tokens : 2 * EDGE + tokens, :] = edge
    beta = column_sum(betas[:, 0, :]) / valid_total
    gamma = column_sum(betas[:, 1, :]) / valid_total
    taps[...] = jnp.zeros(taps.shape, WIDE)
    sums[...] = jnp.zeros(sums.shape, WIDE)
    joint_sum[...] = jnp.zeros(joint_sum.shape, WIDE)
    w3_grad[...] = jnp.zeros(w3_grad.shape, WIDE)
    key_g[...] = jnp.zeros(key_g.shape, WIDE)
    value_g[...] = jnp.zeros(value_g.shape, WIDE)
    wide[1] = jnp.zeros(wide.shape[1:], WIDE)
    wide_pi[...] = jnp.zeros(wide_pi.shape, WIDE)

    standard = (filtered[...] - norm_stats[0:1, :]) * norm_stats[1:2, :]
    valid_all = (row_numbers(0, tokens) < length).astype(WIDE)
    gf = (
        norm_stats[1:2, :]
        * gain_row(small, 5)
        * (shaped_grad[...] - valid_all * (beta + standard * gamma))
    )
    padded_g[EDGE : EDGE + tokens, :] = gf.astype(LOW).astype(WIDE)
    padded[EDGE : EDGE + tokens, :] = gated[...].astype(WIDE)

    @pl.loop(0, tokens // CONV_ROWS)
    def _(at):
        here = padded_g[pl.ds(pl.multiple_of(EDGE + at * CONV_ROWS, 16), CONV_ROWS), :]
        for offset, piece in windows(padded, at * CONV_ROWS, CONV_ROWS):
            product = (piece * here).reshape(CONV_ROWS // 8, 8, width)
            taps[offset - 1] += jnp.sum(product, 0)
        total = jnp.zeros((CONV_ROWS, width), WIDE)
        for offset, piece in windows(padded_g, at * CONV_ROWS, CONV_ROWS):
            total = total + piece * tap_row(small, 31 - offset)
        gx2[rows_at(at, CONV_ROWS), :] = total

    for k in range(31):
        sums[20 + k : 21 + k, :] = column_sum(taps[k])

    @pl.loop(0, tokens // BLOCK)
    def _(at):
        rows = rows_at(at, BLOCK)
        unit2, rate2 = normed(x2[rows, :])
        low2 = (unit2 * gain_row(small, 2) + bias_row(small, 2)).astype(LOW)
        joint = nt(low2, wpi[...]) + pb[...]
        valid = (row_numbers(at * BLOCK, BLOCK) < length).astype(WIDE)
        glu = gx2[rows, :] * valid
        opened = sigmoid(joint[:, width:])
        joint_grad = jnp.concatenate(
            [glu * opened, glu * joint[:, :width] * opened * (1.0 - opened)], 1
        )
        joint_sum[...] += column_sum(joint_grad)
        low_j = joint_grad.astype(LOW)
        wide_pi[...] += tn(low_j, low2)
        gn = nn(low_j, wpi[...])
        sums[2:3, :] += column_sum(gn * unit2)
        sums[8:9, :] += column_sum(gn)
        g2 = gx3[rows, :] + normed_back(gn, unit2, rate2, gain_row(small, 2))
        gx2[rows, :] = g2
        sums[15:16, :] += column_sum(g2)
        low_g = g2.astype(LOW)
        low_a[0, rows, :] = low_g
        mix_grad[rows, :] = nn(low_g, wao[...]).astype(LOW)

    wide[4] = tn(low_a[0], mixed[...])

    @pl.loop(0, tokens // BLOCK)
    def _(at):
        rows = rows_at(at, BLOCK)
        open_keys = lax.broadcasted_iota(jnp.int32, (1, tokens), 1) < length
        sine, cosine = table[rows, :quarter], table[rows, quarter:]
        for head in range(heads):
            cols = slice(head * HEAD, head * HEAD + HEAD)
            scores = head_scores(qkv, wat, table, table_low, rows, cols)
            probs = jnp.where(open_keys, jnp.exp(scores - logs[rows, head : head + 1]), 0.0)
            low_m = mix_grad[rows, cols]
            value_g[:, cols] += tn(probs.astype(LOW), low_m)
            pull = nt(low_m, qkv[3, :, cols])
            delta = jnp.sum(pull * probs, -1, keepdims=True)
            low_s = (probs * (pull - delta)).astype(LOW)
            query_c[rows, cols] = nn(low_s, qkv[2, :, cols]) * eighth
            key_g[:, cols] += tn(low_s, qkv[0, rows, cols]) * eighth
            turned = nn(low_s, table_low[...]) * eighth
            one, two = turned[:, :quarter], turned[:, quarter:]
            lead = jnp.concatenate([two * sine - one * cosine, one * sine + two * cosine], 1)
            low_l = lead.astype(LOW)
            query_p[rows, cols] = nt(low_l, wat[3, cols, :])
            w3_grad[cols, :] += tn(qkv[1, rows, cols], low_l)

    @pl.loop(0, tokens // BLOCK)
    def _(at):
        rows = rows_at(at, BLOCK)
        content, offset = query_c[rows, :], query_p[rows, :]
        query = content + offset
        sums[13:14, :] += column_sum(query)
        sums[14:15, :] += column_sum(value_g[rows, :])
        sums[16:17, :] += column_sum(content)
        sums[17:18, :] += column_sum(offset)
        low_q = query.astype(LOW)
        low_k = key_g[rows, :].astype(LOW)
        low_v = value_g[rows, :].astype(LOW)
        unit1, rate1 = normed(x1[rows, :])
        low_a[0, rows, :] = low_q
        low_a[1, rows, :] = low_k
        low_a[2, rows, :] = low_v
        low_a[3, rows, :] = (unit1 * gain_row(small, 1) + bias_row(small, 1)).astype(LOW)
        gn = nn(low_q, wat[0]) + nn(low_k, wat[1]) + nn(low_v, wat[2])
        sums[1:2, :] += column_sum(gn * unit1)
        sums[7:8, :] += column_sum(gn)
        gx1[rows, :] = gx2[rows, :] + normed_back(gn, unit1, rate1, gain_row(small, 1))

    for k in range(3):
        wide[k] = tn(low_a[k], low_a[3])
    wide[3] = w3_grad[...]
    wide[5] = wpo_grad[...]
    for r in range(32):
        rows = slice(8 * r, 8 * r + 8)
        parts = [wide[k, rows, :] for k in range(5)]
        parts = parts + [wide_pi[16 * r : 16 * r + 16, :], wide[5, rows, :]]
        out[own_b ^ place(r, ORDER_B)] = jnp.concatenate(parts, 0).astype(LOW)


def last_kernel(
    meta, own, other, ga, gx1, small, fb, sums_mid, hidden_mid, betas, sums_back, joint_sum,
    keep, send, out,
    whole, sums, hidden_sum, low_hidden, low_active, low_normed, low_branch, extra, turned,
):
    tokens, width = gx1.shape
    half = keep.shape[0]
    side = meta[0]
    own_a = meta[2]
    fill_whole(meta, own, other, whole)
    sums[...] = sums_back[...]
    hidden_sum[...] = jnp.zeros(hidden_sum.shape, WIDE)
    sums[4:5, :] = sums_mid[0:1, :]
    sums[10:11, :] = sums_mid[1:2, :]
    sums[12:13, :] = sums_mid[2:3, :]
    sums[3:4, :] = sums_mid[3:4, :]
    sums[9:10, :] = sums_mid[4:5, :]
    sums[18:19, :] = sums_mid[5:6, :]
    sums[19:20, :] = betas[0:1, :]
    sums[5:6, :] = betas[1:2, :]

    @pl.loop(0, tokens // BLOCK)
    def _(at):
        rows = rows_at(at, BLOCK)
        unit0, rate0 = normed(whole[rows, :])
        low0 = (unit0 * gain_row(small, 0) + bias_row(small, 0)).astype(LOW)
        low_normed[rows, :] = low0
        w_in, w_out = first_weights(ga)
        hidden = nt(low0, w_in) + fb[0:1, :]
        opened = sigmoid(hidden)
        low_active[rows, :] = (hidden * opened).astype(LOW)
        g1 = gx1[rows, :]
        branch = 0.5 * g1
        sums[11:12, :] += column_sum(branch)
        low_b = branch.astype(LOW)
        low_branch[rows, :] = low_b
        hidden_grad = nt(low_b, w_out) * (opened * (1.0 + hidden * (1.0 - opened)))
        hidden_sum[...] += column_sum(hidden_grad)
        low_h = hidden_grad.astype(LOW)
        low_hidden[rows, :] = low_h
        gn = nn(low_h, w_in)
        sums[0:1, :] += column_sum(gn * unit0)
        sums[6:7, :] += column_sum(gn)
        whole[rows, :] = g1 + normed_back(gn, unit0, rate0, gain_row(small, 0))

    keep[...] = whole[pl.ds(pl.multiple_of(side * half, half), half), :]
    send[...] = whole[pl.ds(pl.multiple_of((1 - side) * half, half), half), :].astype(LOW)
    blocks = out.shape[0]
    out[:, 0:32, :] = tn(low_hidden[...], low_normed[...]).astype(LOW).reshape(blocks, 32, width)
    out[:, 32:64, :] = tn(low_active[...], low_branch[...]).astype(LOW).reshape(blocks, 32, width)
    extra[...] = jnp.zeros(extra.shape, WIDE)
    turned[...] = sums[...].T
    for r in range(32):
        at = own_a ^ place(r, ORDER_A)
        extra[at, 0:8, 0:128] = turned[8 * r : 8 * r + 8, :]
        extra[at, 8:9, 64:80] = joint_sum[0:1, 16 * r : 16 * r + 16]
        at = place(r, ORDER_A)
        c = 32 * place(r, ORDER_C)
        extra[at, 8:9, 0:32] = hidden_sum[0:1, 32 * at : 32 * at + 32]
        extra[at, 8:9, 32:64] = hidden_mid[0:1, c : c + 32]
    out[:, 64:80, :] = extra[...].astype(LOW)


def call(kernel, outs, scratch, *args):
    spec = pl.BlockSpec(memory_space=pltpu.VMEM)
    smem = pl.BlockSpec(memory_space=pltpu.SMEM)
    return pl.pallas_call(
        kernel,
        in_specs=[smem if arg.dtype == jnp.int32 else spec for arg in args],
        out_specs=[spec] * len(outs),
        out_shape=[jax.ShapeDtypeStruct(shape, kind) for shape, kind in outs],
        scratch_shapes=[pltpu.VMEM(shape, kind) for shape, kind in scratch],
        compiler_params=pltpu.CompilerParams(vmem_limit_bytes=60 * 1024 * 1024),
    )(*args)


def fast_body(
    inputs, lengths, cotangent, feed_in, feed_in_bias, feed_out, attend_in, attend_out,
    point_in, point_in_bias, depth_kernel, point_out, gains, biases,
):
    micro_count, seq_count, half, width = inputs.shape
    tokens = half * lax.axis_size("seq")
    valid_total = float(seq_count * lax.axis_size("dp") * tokens * 3 // 4)
    side = lax.axis_index("seq")
    me = lax.axis_index("dp") * 2 + side
    meta = jnp.stack(
        [side, lengths[side, 0], place(me, ORDER_A), place(me, ORDER_B)]
    ).astype(jnp.int32)
    columns = jnp.concatenate(
        [feed_in[0], feed_in[1], attend_in[0], attend_in[1], attend_in[2], attend_in[3],
         attend_out, point_in, point_out], 1,
    ).T
    channel = jnp.pad(
        jnp.concatenate([gains, biases, depth_kernel], 0).T, ((0, 0), (0, width - 51))
    )
    extra_row = jnp.pad(
        jnp.concatenate([feed_in_bias[0], feed_in_bias[1], point_in_bias])[None],
        ((0, 7), (0, width - 80)),
    )
    block_a = jnp.concatenate([columns[0:32], feed_out[0], channel, extra_row], 0)
    block_b = columns[64:128]
    block_c = jnp.concatenate([columns[32:64], feed_out[1]], 0)
    pairs = [(i, 1 - i) for i in range(2)]

    def exchange(value):
        return lax.ppermute(value, "seq", pairs)

    other = exchange(lax.dynamic_index_in_dim(inputs, 1 - side, 0, False)[0])
    ga = gather_chain(block_a, ORDER_A)
    gb = gather_chain(block_b, ORDER_B)
    gc = gather_chain(block_c, ORDER_C)
    other_cot = exchange(lax.dynamic_index_in_dim(cotangent, 1 - side, 0, False)[0])
    table = sinusoid(jnp.arange(tokens, dtype=jnp.int32), width)
    table_low = table.astype(LOW)
    square = (width, width)
    wat, wao, wpi, wpo, small, fb, pb = call(
        prep_kernel,
        [((4,) + square, LOW), (square, LOW), ((2 * width, width), LOW), (square, LOW),
         ((128, width), WIDE), ((2, 1024), WIDE), ((1, 2 * width), WIDE)],
        [((6,) + square, WIDE), ((2 * width, width), WIDE), ((width, 128), WIDE)],
        meta, ga, gb,
    )
    hidden_width = fb.shape[1]
    body_shape = (tokens, width)
    hidden_shape = (tokens, hidden_width)
    pad_shape = (tokens + 2 * EDGE, width)
    x1, qkv, mixed, logs, x2, gated, filtered, stats = call(
        forward_kernel,
        [(body_shape, WIDE), ((4,) + body_shape, LOW), (body_shape, LOW), ((tokens, 128), WIDE),
         (body_shape, WIDE), (body_shape, LOW), (body_shape, WIDE), ((3, width), WIDE)],
        [(body_shape, WIDE), (pad_shape, WIDE)],
        meta, inputs, other, ga, wat, wao, wpi, small, fb, pb, table, table_low,
    )
    dp = lax.axis_size("dp")

    def everywhere(value):
        spread = jnp.broadcast_to(value[None], (dp,) + value.shape)
        return lax.all_to_all(spread, "dp", 0, 0, tiled=True)

    all_stats = everywhere(stats)
    (keep, send, gx3, shaped_grad, norm_stats, sums_mid, hidden_mid, low_hidden, low_active,
     low_normed, low_branch, low_swished, low_third, betas) = call(
        partial(middle_kernel, valid_total),
        [((half, width), LOW), ((half, width), LOW), (body_shape, WIDE), (body_shape, WIDE),
         ((2, width), WIDE), ((8, width), WIDE), ((1, hidden_width), WIDE), (hidden_shape, LOW),
         (hidden_shape, LOW), (body_shape, LOW), (body_shape, LOW), (body_shape, LOW),
         (body_shape, LOW), ((2, width), WIDE)],
        [(body_shape, WIDE), (body_shape, WIDE)],
        meta, cotangent, other_cot, all_stats, filtered, x2, wpo, gc, small, fb,
    )
    all_betas = everywhere(betas)
    arrived_out = exchange(send)
    grads_c, wpo_grad = call(
        outer_kernel, [(gc.shape, LOW), (square, WIDE)], [],
        low_hidden, low_active, low_normed, low_branch, low_swished, low_third,
    )
    shard_c = scatter_chain(grads_c, ORDER_C)
    gx1, grads_b, sums_back, joint_sum = call(
        partial(back_kernel, valid_total),
        [(body_shape, WIDE), (gb.shape, LOW), ((128, width), WIDE), ((1, 2 * width), WIDE)],
        [(pad_shape, WIDE), (pad_shape, WIDE), ((31, 8, width), WIDE), (body_shape, WIDE),
         ((4,) + body_shape, LOW), (body_shape, LOW), (body_shape, WIDE), (body_shape, WIDE),
         (body_shape, WIDE), (body_shape, WIDE), (square, WIDE), ((6,) + square, WIDE),
         ((2 * width, width), WIDE)],
        meta, all_betas, norm_stats, filtered, shaped_grad, gx3, gated, x2, x1, qkv, mixed, logs,
        table, table_low, wat, wao, wpi, small, pb, wpo_grad,
    )
    shard_b = scatter_chain(grads_b, ORDER_B)
    keep_grad, send_grad, grads_a = call(
        last_kernel,
        [((half, width), WIDE), ((half, width), LOW), (ga.shape, LOW)],
        [(body_shape, WIDE), ((128, width), WIDE), ((1, hidden_width), WIDE), (hidden_shape, LOW),
         (hidden_shape, LOW), (body_shape, LOW), (body_shape, LOW), ((32, 16, width), WIDE),
         ((width, 128), WIDE)],
        meta, inputs, other, ga, gx1, small, fb, sums_mid, hidden_mid, betas, sums_back, joint_sum,
    )
    arrived_grad = exchange(send_grad).astype(WIDE)
    shard_a = scatter_chain(grads_a, ORDER_A)

    def both(mine, theirs):
        first = jnp.where(side == 0, mine, theirs)
        second = jnp.where(side == 0, theirs, mine)
        return jnp.stack([first, second])[:, None]

    turned = jnp.concatenate([shard_a[0:32], shard_c[0:32], shard_b], 0).T
    channel = shard_a[64:72, 0:51].T
    row = shard_a[72]
    return (
        both(keep, arrived_out),
        both(keep_grad, arrived_grad),
        jnp.stack([turned[:, 0:32], turned[:, 32:64]]),
        jnp.stack([row[0:32], row[32:64]]),
        jnp.stack([shard_a[32:64], shard_c[32:64]]),
        jnp.stack([turned[:, 64 + 8 * k : 72 + 8 * k] for k in range(4)]),
        turned[:, 96:104],
        turned[:, 104:120],
        row[64:80],
        channel[20:51],
        turned[:, 120:128],
        channel[0:6],
        channel[6:20],
    )


def solution(mesh):
    fast = mesh.shape["seq"] == 2 and mesh.shape["dp"] == 16
    placed = (
        P(None, "dp", "seq", None),
        P(None, "dp"),
        P(None, "dp", "seq", None),
        P(None, None, ("dp", "seq")),
        P(None, ("dp", "seq")),
        P(None, ("dp", "seq"), None),
        P(None, None, ("dp", "seq")),
        P(None, ("dp", "seq")),
        P(None, ("dp", "seq")),
        P(("dp", "seq")),
        P(None, ("dp", "seq")),
        P(None, ("dp", "seq")),
        P(None, ("dp", "seq")),
        P(None, ("dp", "seq")),
    )
    return jax.shard_map(
        fast_body if fast else body,
        mesh=mesh,
        in_specs=placed,
        out_specs=(
            P(None, "dp", "seq", None),
            P(None, "dp", "seq", None),
            P(None, None, ("dp", "seq")),
            P(None, ("dp", "seq")),
            P(None, ("dp", "seq"), None),
            P(None, None, ("dp", "seq")),
            P(None, ("dp", "seq")),
            P(None, ("dp", "seq")),
            P(("dp", "seq")),
            P(None, ("dp", "seq")),
            P(None, ("dp", "seq")),
            P(None, ("dp", "seq")),
            P(None, ("dp", "seq")),
        ),
        check_vma=False,
    )
```
